512 devices in a mesh: dst: 32 (over z, core), src: 16 (over y, x).
Axes of the slice: x: 4, y: 4, z: 16, core: 2. Of those that a mesh axis runs over, the one named last changes fastest.
Arguments:
- adj_tiles: bfloat16 [32, 16, 64, 64, 512], P('dst', 'src'), may hold values from 0 to 0.011047363
- tile_cols: int32 [32, 16, 64, 8], P('dst', 'src'), may hold values from 0 to 63
- send_block: int32 [32, 16, 32, 2], P('dst', 'src'), may hold values from 0 to 15
- send_count: int32 [32, 16, 32], P('dst', 'src'), may hold values from 1 to 2, as said below
- history: bfloat16 [64, 16, 8192], P('dst', 'src'), may hold values from -6 to 6
- node_feats: bfloat16 [512, 8192], P('dst', 'src'), may hold values from -6 to 6
- w_neigh: bfloat16 [128, 128], replicated, may hold values from -0.5 to 0.5
- w_self: bfloat16 [128, 128], replicated, may hold values from -0.5 to 0.5
- out_bias: float32 [128], replicated, may hold values from -3 to 3
- cotangent: bfloat16 [512, 8192], P('dst', 'src'), may hold values from -6 to 6
Outputs:
- new_embed: bfloat16 [512, 8192], P('dst', 'src')
- grad_neigh: float32 [128, 128], replicated
- grad_self: float32 [128, 128], replicated
- grad_bias: float32 [128], replicated
The draws below stay inside these ranges and needn't reach their ends.
Inputs may be any that keep to these rules, and one draw needn't show every extreme that they name: `send_count`: in every draw, for each source group some owner gets 2 live slots from every device of that group.
All inputs are finite; a program needn't handle non-finite values.
Results may differ from the reference program's by a relative error of at most 0.0052.
Values may be sent and summed in bfloat16 or wider, within the bound.
A program may use at most 64 MiB of HBM per device.

```python
import jax
import jax.numpy as jnp
from jax import lax

BLK = 64
F = 128
TPS = 8
SLOT_DEV = 64
OWN_DEV = 16
OWNERS = 32
GROUPS = 16
CAP = 2
GB = 64
RB = 512


def draw_send_count(key, part):
    inner = jax.random.fold_in(key, 11)
    first_key, second_key = jax.random.split(inner)
    base = jax.random.randint(first_key, (OWNERS, GROUPS, OWNERS), 1, CAP + 1)
    full_peer = jax.random.randint(second_key, (GROUPS,), 0, OWNERS)
    hit_mask = jnp.arange(OWNERS)[None, None, :] == full_peer[None, :, None]
    return jnp.where(hit_mask, CAP, base).astype(jnp.int32)


def set_ends(array, own_key, least, top_value):
    longest = array.shape.index(max(array.shape))
    spots = []
    for shift in (0, 1):
        where = [jax.random.randint(jax.random.fold_in(own_key, axis), (), 0, length) for axis, length in enumerate(array.shape)]
        where[longest] = (where[longest] + shift) % array.shape[longest]
        spots.append(tuple(where))
    return array.at[spots[0]].set(least).at[spots[1]].set(top_value)


def block_scale(rng, extent, shards, least, top_value):
    gain = 1.0
    for position, blocks in shards:
        draws = jax.random.uniform(jax.random.fold_in(jax.random.fold_in(rng, 6), position), (blocks,), jnp.float32, least / len(shards), top_value / len(shards))
        gain = gain * jnp.repeat(jnp.exp(draws), extent[position] // blocks).reshape((-1,) + (1,) * (len(extent) - 1 - position))
    return gain


def bell_draw(rng, dims, deviation, most, cuts=(), kind=jnp.bfloat16):
    values = jax.random.normal(rng, dims, jnp.float32) * deviation
    if len(cuts) > 0:
        values = block_scale(rng, dims, cuts, -0.22, 0.18) * values
    return jnp.clip(values, min=-most, max=most).astype(kind)


def setup_inputs(seed: int = 0) -> dict:
    seeds = jax.random.split(jax.random.key(seed), 11)
    return {
        "adj_tiles": jnp.clip(0.011047363 * jax.random.uniform(seeds[0], (OWNERS, GROUPS, SLOT_DEV, BLK, TPS * BLK), jnp.float32) ** block_scale(seeds[0], (OWNERS, GROUPS, SLOT_DEV, BLK, TPS * BLK), ((0, 32), (1, 16)), -0.2, 0.2), 0.0, 0.011047363).astype(jnp.bfloat16),
        "tile_cols": set_ends(jax.random.randint(seeds[1], (OWNERS, GROUPS, SLOT_DEV, TPS), 0, GB), jax.random.fold_in(seeds[1], 1), 0, GB - 1).astype(jnp.int32),
        "send_block": set_ends(jax.random.randint(seeds[2], (OWNERS, GROUPS, OWNERS, CAP), 0, OWN_DEV), jax.random.fold_in(seeds[2], 1), 0, OWN_DEV - 1).astype(jnp.int32),
        "send_count": draw_send_count(jax.random.fold_in(seeds[10], 71), 0),
        "history": bell_draw(seeds[4], (GB, GROUPS, BLK * F), 1.0, 6.0, ((0, 32), (1, 16))),
        "node_feats": bell_draw(seeds[5], (RB, BLK * F), 1.0, 6.0, ((0, 32), (1, 16))),
        "w_neigh": bell_draw(seeds[6], (F, F), F ** -0.5, 0.5),
        "w_self": bell_draw(seeds[7], (F, F), F ** -0.5, 0.5),
        "out_bias": bell_draw(seeds[8], (F,), 0.5, 3.0, (), jnp.float32),
        "cotangent": bell_draw(seeds[9], (RB, BLK * F), 1.0, 6.0, ((0, 32), (1, 16))),
    }


def reference(adj_tiles, tile_cols, send_block, send_count, history, node_feats, w_neigh, w_self, out_bias, cotangent):
    devices = OWNERS * GROUPS
    capacity = SLOT_DEV // OWNERS
    tiles_all = adj_tiles.reshape(devices, SLOT_DEV, BLK, TPS * BLK)
    cols_all = tile_cols.reshape(devices, SLOT_DEV * TPS).astype(jnp.int32)
    blocks_all = send_block.reshape(devices, OWNERS, capacity).astype(jnp.int32)
    counts_all = send_count.reshape(devices, OWNERS).astype(jnp.int32)
    group_ids = (jnp.arange(devices) % GROUPS).astype(jnp.int32)

    def step(agg, inputs):
        tiles_one, cols_one, blocks_one, counts_one, group_id = inputs
        group_table = lax.dynamic_index_in_dim(history, group_id, axis=1, keepdims=False)
        group_table = group_table.reshape(GB, BLK, F)
        picked = group_table[cols_one].reshape(SLOT_DEV, TPS * BLK, F)
        partial_value = jnp.einsum("sir,srf->sif", tiles_one.astype(jnp.float32), picked.astype(jnp.float32), precision=lax.Precision.HIGHEST)
        alive_mask = (jnp.arange(capacity)[None, :] < counts_one[:, None]).astype(jnp.float32)
        partial_value = partial_value.reshape(OWNERS, capacity, BLK * F) * alive_mask[:, :, None]
        target_rows = (jnp.arange(OWNERS, dtype=jnp.int32)[:, None] * OWN_DEV + blocks_one).reshape(-1)
        agg = agg.at[target_rows].add(partial_value.reshape(-1, BLK * F))
        return agg, None

    agg0 = jnp.zeros((RB, BLK * F), jnp.float32)
    agg, _ = lax.scan(step, agg0, (tiles_all, cols_all, blocks_all, counts_all, group_ids))
    agg_rows = agg.astype(jnp.bfloat16).reshape(RB * BLK, F)
    self_rows = node_feats.reshape(RB * BLK, F)
    pre_act = jnp.dot(agg_rows, w_neigh, preferred_element_type=jnp.float32) + jnp.dot(self_rows, w_self, preferred_element_type=jnp.float32) + out_bias
    sigmoid_z = jax.nn.sigmoid(pre_act)
    new_embed = (pre_act * sigmoid_z).astype(jnp.bfloat16).reshape(RB, BLK * F)
    loss_scale = float(RB * BLK) ** -0.5
    slope = sigmoid_z * (1.0 + pre_act * (1.0 - sigmoid_z))
    grad_pre = cotangent.reshape(RB * BLK, F).astype(jnp.float32) * slope * loss_scale
    grad_low = grad_pre.astype(jnp.bfloat16)
    grad_neigh = jnp.dot(agg_rows.T, grad_low, preferred_element_type=jnp.float32)
    grad_self = jnp.dot(self_rows.T, grad_low, preferred_element_type=jnp.float32)
    grad_bias = jnp.sum(grad_pre, axis=0)
    return (new_embed, grad_neigh, grad_self, grad_bias)
```

```python
import jax
import jax.numpy as jnp
from jax import lax
from jax.experimental import pallas as pl
from jax.experimental.pallas import tpu as pltpu
from jax.sharding import PartitionSpec as P

MESH = pl.DeviceIdType.MESH
NZ, NC, NS = 16, 2, 16
NP = NC * NS
BLK, F, TPS, SLOTS, OWN, NJ = 64, 128, 8, 64, 16, 4
HZ = NZ // 2
LANES = 128
TREE = (
    (0, (3, -3, 1, -1)),
    (3, (3, -1, 1)),
    (-3, (-3, 1, -1)),
    (6, (2, 1, -1)),
    (-6, (-1, 1)),
    (1, ()),
    (-1, ()),
    (2, ()),
    (-2, ()),
    (4, ()),
    (-4, ()),
    (5, ()),
    (-5, ()),
    (7, ()),
    (-7, ()),
    (8, ()),
)
NEAR = (1, -1, 2, -2, 3, -3)
F32, BF16 = jnp.float32, jnp.bfloat16


def body(
    cols,
    adj_hbm,
    hist_hbm,
    ids_hbm,
    feats_hbm,
    cot_hbm,
    wn_hbm,
    ws_hbm,
    bias_hbm,
    emb_ref,
    gn_ref,
    gs_ref,
    gb_ref,
    adj,
    table,
    ids,
    feats,
    cot,
    wn,
    ws,
    bias,
    part,
    outbox,
    inbox,
    idbox,
    zout,
    zin,
    grad,
    gbias,
    gin,
    gbin,
    gsum,
    gbsum,
    gzin,
    gbzin,
    gfin,
    gall,
    load_sem,
    adj_sem,
    table_sem,
    table_in,
    pair_in,
    send_sem,
    in_sem,
    id_sem,
    z_sem,
    g_sem,
    gb_sem,
    gz_sem,
    gbz_sem,
    ga_sem,
):
    d = lax.axis_index("dst")
    s = lax.axis_index("src")
    z = d // NC
    c = d % NC
    me = c * NS + s

    def plane(i):
        return (z * NC + i // NS, i % NS)

    def at_z(t):
        return (t * NC + c, s)

    small = [
        pltpu.make_async_copy(a, b, load_sem.at[n])
        for n, (a, b) in enumerate(
            (
                (ids_hbm, ids),
                (feats_hbm, feats),
                (cot_hbm, cot),
                (wn_hbm, wn),
                (ws_hbm, ws),
                (bias_hbm, bias),
            )
        )
    ]
    own = pltpu.make_async_copy(hist_hbm, table.at[pl.ds(d * 2, 2)], table_sem)
    own.start()
    big = pltpu.make_async_copy(adj_hbm, adj, adj_sem)

    barrier = pltpu.get_barrier_semaphore()
    for off in NEAR:
        pl.semaphore_signal(
            barrier, inc=1, device_id=at_z((z + off + NZ) % NZ), device_id_type=MESH
        )

    def greet(k, carry):
        pl.semaphore_signal(
            barrier, inc=1, device_id=plane((me + k) % NP), device_id_type=MESH
        )
        return carry

    lax.fori_loop(1, NP, greet, 0)
    for op in small:
        op.start()
    big.start()
    own.wait()
    pl.semaphore_wait(barrier, NP - 1 + len(NEAR))

    slot_of = {off: n for n, (off, _) in enumerate(TREE)}

    def block(off):
        return table.at[pl.ds(((z - off + NZ) % NZ) * (2 * NC) + c * 2, 2)]

    def wire(off, step):
        landing = off + step
        return pltpu.make_async_remote_copy(
            src_ref=block(off),
            dst_ref=block(off),
            send_sem=send_sem.at[0],
            recv_sem=table_in.at[slot_of[landing]],
            device_id=at_z((z + step + NZ) % NZ),
            device_id_type=MESH,
        )

    def twin(off):
        return pltpu.make_async_remote_copy(
            src_ref=block(off),
            dst_ref=block(off),
            send_sem=send_sem.at[0],
            recv_sem=pair_in,
            device_id=(z * NC + 1 - c, s),
            device_id_type=MESH,
        )

    for off, moves in TREE:
        if off != 0:
            pltpu.make_async_copy(block(off), block(off), table_in.at[slot_of[off]]).wait()
        for step in moves:
            wire(off, step).start()
        twin(off).start()

    small[0].wait()

    def send_ids(k, carry):
        i = (me + k) % NP
        pltpu.make_async_remote_copy(
            src_ref=ids.at[i // NS],
            dst_ref=idbox.at[me],
            send_sem=send_sem.at[1],
            recv_sem=id_sem,
            device_id=plane(i),
            device_id_type=MESH,
        ).start()
        return carry

    lax.fori_loop(1, NP, send_ids, 0)
    pltpu.make_async_copy(ids.at[c], idbox.at[me], id_sem).start()

    big.wait()
    pltpu.make_async_copy(
        table.at[pl.ds(0, 2 * NZ)], table.at[pl.ds(0, 2 * NZ)], pair_in
    ).wait()

    for h in range(2):

        def slot(n, carry):
            q = (n // 4) * 8 + h * 4 + n % 4
            picked = jnp.concatenate([table[cols[q, t]] for t in range(TPS)], axis=0)
            part[n] = jnp.dot(adj[q], picked, preferred_element_type=F32)
            return carry

        lax.fori_loop(0, SLOTS // 2, slot, 0, unroll=4)

        def pack(i, carry):
            for j in range(NJ):
                row = (i % NS) * NJ + j
                two = [
                    part[pl.ds((i // NS) * 2 + k, HZ, stride=4), row, :] for k in range(2)
                ]
                outbox[h, i, j] = jnp.concatenate(two, axis=0).astype(BF16)
            return carry

        lax.fori_loop(0, NP, pack, 0)

        def send(k, carry):
            i = (me + k) % NP
            pltpu.make_async_remote_copy(
                src_ref=outbox.at[h, i],
                dst_ref=inbox.at[h, me],
                send_sem=send_sem.at[2],
                recv_sem=in_sem.at[h],
                device_id=plane(i),
                device_id_type=MESH,
            ).start()
            return carry

        lax.fori_loop(1, NP, send, 0)
        pltpu.make_async_copy(outbox.at[h, me], inbox.at[h, me], in_sem.at[h]).start()

    for op in small[1:]:
        op.wait()

    pltpu.make_async_copy(idbox, idbox, id_sem).wait()
    lane_dev = lax.broadcasted_iota(jnp.int32, (1, LANES), 1) // 16
    row_id = lax.broadcasted_iota(jnp.int32, (LANES, LANES), 0)
    for h in range(2):
        parts = []
        for g in range(NP // 8):
            row = jnp.zeros((1, LANES), jnp.int32)
            for n in range(8):
                row = jnp.where(lane_dev == n, idbox[g * 8 + n, pl.ds(h, 1), :], row)
            parts.append((row_id == row).astype(F32).astype(BF16))
        chosen = jnp.concatenate(parts, axis=1)
        pltpu.make_async_copy(inbox.at[h], inbox.at[h], in_sem.at[h]).wait()
        for j in range(NJ):
            got = inbox[h, :, j].reshape(NP * 16, F)
            total = jnp.dot(chosen, got, preferred_element_type=F32)
            zout[h, :, j] = total.astype(BF16).reshape(HZ, OWN, F)
        for i in range(HZ):
            t = 2 * i + h

            @pl.when(t != z)
            def _():
                pltpu.make_async_remote_copy(
                    src_ref=zout.at[h, i],
                    dst_ref=zin.at[z],
                    send_sem=send_sem.at[3],
                    recv_sem=z_sem,
                    device_id=at_z(t),
                    device_id_type=MESH,
                ).start()

            @pl.when(t == z)
            def _():
                pltpu.make_async_copy(zout.at[h, i], zin.at[z], z_sem).start()

    pltpu.make_async_copy(zin, zin, z_sem).wait()

    aggs, selfs, grads_low = [], [], []
    gbias_sum = jnp.zeros((1, F), F32)
    for j in range(NJ):
        agg = zin[0, j].astype(F32)
        for t in range(1, NZ):
            agg = agg + zin[t, j].astype(F32)
        agg = agg.astype(BF16)
        mine = feats[:, j * F : (j + 1) * F]
        pre = (
            jnp.dot(agg, wn[...], preferred_element_type=F32)
            + jnp.dot(mine, ws[...], preferred_element_type=F32)
            + bias[...]
        )
        sig = jax.nn.sigmoid(pre)
        emb_ref[:, j * F : (j + 1) * F] = (pre * sig).astype(BF16)
        slope = sig * (1.0 + pre * (1.0 - sig))
        gpre = cot[:, j * F : (j + 1) * F].astype(F32) * slope * (float(NZ * NC * OWN * BLK) ** -0.5)
        gbias_sum = gbias_sum + jnp.sum(gpre, axis=0, keepdims=True)
        aggs.append(agg)
        selfs.append(mine)
        grads_low.append(gpre.astype(BF16))
    low = jnp.concatenate(grads_low, axis=0)
    for n, left in enumerate((aggs, selfs)):
        left = jnp.concatenate(left, axis=0)
        prod = lax.dot_general(
            left, low, (((0,), (0,)), ((), ())), preferred_element_type=F32
        )
        grad[pl.ds(n * 16, 16)] = prod.reshape(16, 8, F)
    gbias[...] = gbias_sum

    def scatter(k, carry):
        i = (me + k) % NP
        pltpu.make_async_remote_copy(
            src_ref=grad.at[i],
            dst_ref=gin.at[me],
            send_sem=send_sem.at[4],
            recv_sem=g_sem,
            device_id=plane(i),
            device_id_type=MESH,
        ).start()
        pltpu.make_async_remote_copy(
            src_ref=gbias,
            dst_ref=gbin.at[me],
            send_sem=send_sem.at[5],
            recv_sem=gb_sem,
            device_id=plane(i),
            device_id_type=MESH,
        ).start()
        return carry

    lax.fori_loop(1, NP, scatter, 0)
    pltpu.make_async_copy(grad.at[me], gin.at[me], g_sem).start()
    pltpu.make_async_copy(gbias, gbin.at[me], gb_sem).start()
    pltpu.make_async_copy(gin, gin, g_sem).wait()
    pltpu.make_async_copy(gbin, gbin, gb_sem).wait()
    total, btotal = gin[0], gbin[0]
    for i in range(1, NP):
        total = total + gin[i]
        btotal = btotal + gbin[i]
    gsum[...] = total
    gbsum[...] = btotal

    def along(k, carry):
        t = (z + k) % NZ
        pltpu.make_async_remote_copy(
            src_ref=gsum,
            dst_ref=gzin.at[z],
            send_sem=send_sem.at[6],
            recv_sem=gz_sem,
            device_id=at_z(t),
            device_id_type=MESH,
        ).start()
        pltpu.make_async_remote_copy(
            src_ref=gbsum,
            dst_ref=gbzin.at[z],
            send_sem=send_sem.at[7],
            recv_sem=gbz_sem,
            device_id=at_z(t),
            device_id_type=MESH,
        ).start()
        return carry

    lax.fori_loop(1, NZ, along, 0)
    pltpu.make_async_copy(gsum, gzin.at[z], gz_sem).start()
    pltpu.make_async_copy(gbsum, gbzin.at[z], gbz_sem).start()
    pltpu.make_async_copy(gzin, gzin, gz_sem).wait()
    pltpu.make_async_copy(gbzin, gbzin, gbz_sem).wait()
    total, btotal = gzin[0], gbzin[0]
    for t in range(1, NZ):
        total = total + gzin[t]
        btotal = btotal + gbzin[t]
    gfin[...] = total
    gb_ref[...] = btotal

    def gather(k, carry):
        pltpu.make_async_remote_copy(
            src_ref=gfin,
            dst_ref=gall.at[me],
            send_sem=send_sem.at[8],
            recv_sem=ga_sem,
            device_id=plane((me + k) % NP),
            device_id_type=MESH,
        ).start()
        return carry

    lax.fori_loop(1, NP, gather, 0)
    pltpu.make_async_copy(gfin, gall.at[me], ga_sem).start()
    pltpu.make_async_copy(gall, gall, ga_sem).wait()
    gn_ref[...] = gall[pl.ds(0, 16)].reshape(F, F)
    gs_ref[...] = gall[pl.ds(16, 16)].reshape(F, F)

    def sent(n, ref):
        pltpu.make_async_copy(ref, ref, send_sem.at[n]).wait()

    sent(0, table.at[pl.ds(0, 2 * (2 * NZ - 1))])
    sent(1, idbox.at[pl.ds(0, NP - 1)])
    for _ in range(2):
        sent(2, inbox.at[0, pl.ds(0, NP - 1)])
    sent(3, zin.at[pl.ds(0, NZ - 1)])
    sent(4, gin.at[pl.ds(0, NP - 1)])
    sent(5, gbin.at[pl.ds(0, NP - 1)])
    sent(6, gzin.at[pl.ds(0, NZ - 1)])
    sent(7, gbzin.at[pl.ds(0, NZ - 1)])
    sent(8, gall.at[pl.ds(0, NP - 1)])


def on_device(
    adj_tiles,
    tile_cols,
    send_block,
    send_count,
    history,
    node_feats,
    w_neigh,
    w_self,
    out_bias,
    cotangent,
):
    adj = adj_tiles.reshape(SLOTS, BLK, TPS * BLK)
    cols = tile_cols.reshape(SLOTS, TPS)
    hist = history.reshape(2, BLK, F)
    count = send_count.reshape(HZ, 2, NC, 1)
    dest = send_block.reshape(HZ, 2, NC, 2)
    alive = jnp.arange(2)[None, None, None, :] < count
    ids = jnp.where(alive, dest + jnp.arange(HZ)[:, None, None, None] * OWN, -1)
    ids = ids.transpose(2, 1, 3, 0).reshape(NC, 2, 16)
    ids = jnp.tile(ids, (1, 1, LANES // 16))
    any_spec = pl.BlockSpec(memory_space=pl.ANY)
    vmem_spec = pl.BlockSpec(memory_space=pltpu.VMEM)
    dma = pltpu.SemaphoreType.DMA
    emb, gn, gs, gb = pl.pallas_call(
        body,
        out_shape=(
            jax.ShapeDtypeStruct(node_feats.shape, BF16),
            jax.ShapeDtypeStruct((F, F), F32),
            jax.ShapeDtypeStruct((F, F), F32),
            jax.ShapeDtypeStruct((1, F), F32),
        ),
        in_specs=[pl.BlockSpec(memory_space=pltpu.SMEM)] + [any_spec] * 8,
        out_specs=(vmem_spec,) * 4,
        scratch_shapes=[
            pltpu.VMEM((SLOTS, BLK, TPS * BLK), BF16),
            pltpu.VMEM((2 * NC * NZ, BLK, F), BF16),
            pltpu.VMEM((NC, 2, LANES), jnp.int32),
            pltpu.VMEM(node_feats.shape, BF16),
            pltpu.VMEM(node_feats.shape, BF16),
            pltpu.VMEM((F, F), BF16),
            pltpu.VMEM((F, F), BF16),
            pltpu.VMEM((1, F), F32),
            pltpu.VMEM((SLOTS // 2, BLK, F), F32),
            pltpu.VMEM((2, NP, NJ, 16, F), BF16),
            pltpu.VMEM((2, NP, NJ, 16, F), BF16),
            pltpu.VMEM((NP, 2, LANES), jnp.int32),
            pltpu.VMEM((2, HZ, NJ, OWN, F), BF16),
            pltpu.VMEM((NZ, NJ, OWN, F), BF16),
            pltpu.VMEM((NP, 8, F), F32),
            pltpu.VMEM((1, F), F32),
            pltpu.VMEM((NP, 8, F), F32),
            pltpu.VMEM((NP, 1, F), F32),
            pltpu.VMEM((8, F), F32),
            pltpu.VMEM((1, F), F32),
            pltpu.VMEM((NZ, 8, F), F32),
            pltpu.VMEM((NZ, 1, F), F32),
            pltpu.VMEM((8, F), F32),
            pltpu.VMEM((NP, 8, F), F32),
            dma((6,)),
            dma,
            dma,
            dma((NZ,)),
            dma,
            dma((9,)),
            dma((2,)),
            dma,
            dma,
            dma,
            dma,
            dma,
            dma,
            dma,
        ],
        compiler_params=pltpu.CompilerParams(collective_id=0, has_side_effects=True),
    )(
        cols,
        adj,
        hist,
        ids,
        node_feats,
        cotangent,
        w_neigh,
        w_self,
        out_bias.reshape(1, F),
    )
    return emb, gn, gs, gb.reshape(F)


def solution(mesh):
    in_specs = (
        P("dst", "src", None, None, None),
        P("dst", "src", None, None),
        P("dst", "src", None, None),
        P("dst", "src", None),
        P("dst", "src", None),
        P("dst", "src"),
        P(),
        P(),
        P(),
        P("dst", "src"),
    )
    out_specs = (P("dst", "src"), P(), P(), P())
    return jax.shard_map(
        on_device, mesh=mesh, in_specs=in_specs, out_specs=out_specs, check_vma=False
    )
```

```python
import jax
import jax.numpy as jnp
from jax import lax
from jax.experimental import pallas as pl
from jax.experimental.pallas import tpu as pltpu
from jax.sharding import PartitionSpec as P

MESH = pl.DeviceIdType.MESH
NZ, NC, NS = 16, 2, 16
NP = NC * NS
BLK, F, TPS, SLOTS, OWN, NJ = 64, 128, 8, 64, 16, 4
HZ = NZ // 2
LANES = 128
TREE = (
    (0, (3, -3, 1, -1)),
    (3, (3, -1, 1)),
    (-3, (-3, 1, -1)),
    (6, (2, 1, -1)),
    (-6, (-1, 1)),
    (1, ()),
    (-1, ()),
    (2, ()),
    (-2, ()),
    (4, ()),
    (-4, ()),
    (5, ()),
    (-5, ()),
    (7, ()),
    (-7, ()),
    (8, ()),
)
NEAR = (1, -1, 2, -2, 3, -3)
F32, BF16 = jnp.float32, jnp.bfloat16


def body(
    cols_hbm,
    block_hbm,
    count_hbm,
    adj_hbm,
    hist_hbm,
    feats_hbm,
    cot_hbm,
    wn_hbm,
    ws_hbm,
    bias_hbm,
    emb_ref,
    grads_ref,
    gb_ref,
    cols,
    blocks,
    counts,
    adj,
    hist,
    table,
    ids,
    feats,
    cot,
    wn,
    ws,
    bias,
    part,
    outbox,
    inbox,
    idbox,
    zout,
    zin,
    grad,
    gbias,
    gin,
    gbin,
    gsum,
    gbsum,
    gzin,
    gbzin,
    gfin,
    gall,
    load_sem,
    adj_sem,
    table_sem,
    table_in,
    pair_in,
    send_sem,
    in_sem,
    id_sem,
    z_sem,
    g_sem,
    gb_sem,
    gz_sem,
    gbz_sem,
    ga_sem,
):
    d = lax.axis_index("dst")
    s = lax.axis_index("src")
    z = d // NC
    c = d % NC
    me = c * NS + s

    def plane(i):
        return (z * NC + i // NS, i % NS)

    def at_z(t):
        return (t * NC + c, s)

    small = [
        pltpu.make_async_copy(a, b, load_sem.at[n])
        for n, (a, b) in enumerate(
            (
                (cols_hbm, cols),
                (block_hbm, blocks),
                (count_hbm, counts),
                (feats_hbm, feats),
                (cot_hbm, cot),
                (wn_hbm, wn),
                (ws_hbm, ws),
                (bias_hbm, bias),
            )
        )
    ]
    own = pltpu.make_async_copy(hist_hbm, hist, table_sem)
    own.start()
    big = pltpu.make_async_copy(adj_hbm, adj, adj_sem)

    barrier = pltpu.get_barrier_semaphore()
    for off in NEAR:
        pl.semaphore_signal(
            barrier, inc=1, device_id=at_z((z + off + NZ) % NZ), device_id_type=MESH
        )

    def greet(k, carry):
        pl.semaphore_signal(
            barrier, inc=1, device_id=plane((me + k) % NP), device_id_type=MESH
        )
        return carry

    lax.fori_loop(1, NP, greet, 0)
    for op in small:
        op.start()
    big.start()
    own.wait()
    for g in range(2):
        table[d * 2 + g] = hist[:, g, :]
    for op in small[:3]:
        op.wait()
    lane_slot = lax.broadcasted_iota(jnp.int32, (1, LANES), 1) % 16
    for core in range(NC):
        for h in range(2):
            row = jnp.full((1, LANES), -1, jnp.int32)
            for n in range(16):
                k, i = n // HZ, n % HZ
                p = (2 * i + h) * NC + core
                value = jnp.where(counts[0, p] > k, blocks[k, p] + i * OWN, -1)
                row = jnp.where(lane_slot == n, value, row)
            ids[core, pl.ds(h, 1), :] = row
    pl.semaphore_wait(barrier, NP - 1 + len(NEAR))

    slot_of = {off: n for n, (off, _) in enumerate(TREE)}

    def block(off):
        return table.at[pl.ds(((z - off + NZ) % NZ) * (2 * NC) + c * 2, 2)]

    def wire(off, step):
        landing = off + step
        return pltpu.make_async_remote_copy(
            src_ref=block(off),
            dst_ref=block(off),
            send_sem=send_sem.at[0],
            recv_sem=table_in.at[slot_of[landing]],
            device_id=at_z((z + step + NZ) % NZ),
            device_id_type=MESH,
        )

    def twin(off):
        return pltpu.make_async_remote_copy(
            src_ref=block(off),
            dst_ref=block(off),
            send_sem=send_sem.at[0],
            recv_sem=pair_in,
            device_id=(z * NC + 1 - c, s),
            device_id_type=MESH,
        )

    for off, moves in TREE:
        if off != 0:
            pltpu.make_async_copy(block(off), block(off), table_in.at[slot_of[off]]).wait()
        for step in moves:
            wire(off, step).start()
        twin(off).start()

    def send_ids(k, carry):
        i = (me + k) % NP
        pltpu.make_async_remote_copy(
            src_ref=ids.at[i // NS],
            dst_ref=idbox.at[me],
            send_sem=send_sem.at[1],
            recv_sem=id_sem,
            device_id=plane(i),
            device_id_type=MESH,
        ).start()
        return carry

    lax.fori_loop(1, NP, send_ids, 0)
    pltpu.make_async_copy(ids.at[c], idbox.at[me], id_sem).start()

    big.wait()
    pltpu.make_async_copy(
        table.at[pl.ds(0, 2 * NZ)], table.at[pl.ds(0, 2 * NZ)], pair_in
    ).wait()

    for h in range(2):

        def slot(n, carry):
            q = (n // 4) * 8 + h * 4 + n % 4
            picked = jnp.concatenate([table[cols[t, q]] for t in range(TPS)], axis=0)
            part[n] = jnp.dot(adj[q], picked, preferred_element_type=F32)
            return carry

        lax.fori_loop(0, SLOTS // 2, slot, 0, unroll=4)

        def pack(i, carry):
            for j in range(NJ):
                row = (i % NS) * NJ + j
                two = [
                    part[pl.ds((i // NS) * 2 + k, HZ, stride=4), row, :] for k in range(2)
                ]
                outbox[h, i, j] = jnp.concatenate(two, axis=0).astype(BF16)
            return carry

        lax.fori_loop(0, NP, pack, 0)

        def send(k, carry):
            i = (me + k) % NP
            pltpu.make_async_remote_copy(
                src_ref=outbox.at[h, i],
                dst_ref=inbox.at[h, me],
                send_sem=send_sem.at[2],
                recv_sem=in_sem.at[h],
                device_id=plane(i),
                device_id_type=MESH,
            ).start()
            return carry

        lax.fori_loop(1, NP, send, 0)
        pltpu.make_async_copy(outbox.at[h, me], inbox.at[h, me], in_sem.at[h]).start()

    for op in small[3:]:
        op.wait()

    pltpu.make_async_copy(idbox, idbox, id_sem).wait()
    lane_dev = lax.broadcasted_iota(jnp.int32, (1, LANES), 1) // 16
    row_id = lax.broadcasted_iota(jnp.int32, (LANES, LANES), 0)
    for h in range(2):
        parts = []
        for g in range(NP // 8):
            row = jnp.zeros((1, LANES), jnp.int32)
            for n in range(8):
                row = jnp.where(lane_dev == n, idbox[g * 8 + n, pl.ds(h, 1), :], row)
            parts.append((row_id == row).astype(F32).astype(BF16))
        chosen = jnp.concatenate(parts, axis=1)
        pltpu.make_async_copy(inbox.at[h], inbox.at[h], in_sem.at[h]).wait()
        for j in range(NJ):
            got = inbox[h, :, j].reshape(NP * 16, F)
            total = jnp.dot(chosen, got, preferred_element_type=F32)
            zout[h, :, j] = total.astype(BF16).reshape(HZ, OWN, F)
        for i in range(HZ):
            t = 2 * i + h

            @pl.when(t != z)
            def _():
                pltpu.make_async_remote_copy(
                    src_ref=zout.at[h, i],
                    dst_ref=zin.at[z],
                    send_sem=send_sem.at[3],
                    recv_sem=z_sem,
                    device_id=at_z(t),
                    device_id_type=MESH,
                ).start()

            @pl.when(t == z)
            def _():
                pltpu.make_async_copy(zout.at[h, i], zin.at[z], z_sem).start()

    pltpu.make_async_copy(zin, zin, z_sem).wait()

    aggs, selfs, grads_low = [], [], []
    gbias_sum = jnp.zeros((1, F), F32)
    for j in range(NJ):
        agg = zin[0, j].astype(F32)
        for t in range(1, NZ):
            agg = agg + zin[t, j].astype(F32)
        agg = agg.astype(BF16)
        mine = feats[:, j * F : (j + 1) * F]
        pre = (
            jnp.dot(agg, wn[...], preferred_element_type=F32)
            + jnp.dot(mine, ws[...], preferred_element_type=F32)
            + bias[...]
        )
        sig = jax.nn.sigmoid(pre)
        emb_ref[:, j * F : (j + 1) * F] = (pre * sig).astype(BF16)
        slope = sig * (1.0 + pre * (1.0 - sig))
        gpre = cot[:, j * F : (j + 1) * F].astype(F32) * slope * (float(NZ * NC * OWN * BLK) ** -0.5)
        gbias_sum = gbias_sum + jnp.sum(gpre, axis=0, keepdims=True)
        aggs.append(agg)
        selfs.append(mine)
        grads_low.append(gpre.astype(BF16))
    low = jnp.concatenate(grads_low, axis=0)
    for n, left in enumerate((aggs, selfs)):
        left = jnp.concatenate(left, axis=0)
        prod = lax.dot_general(
            left, low, (((0,), (0,)), ((), ())), preferred_element_type=F32
        )
        grad[pl.ds(n * 16, 16)] = prod.reshape(16, 8, F)
    gbias[...] = gbias_sum

    def scatter(k, carry):
        i = (me + k) % NP
        pltpu.make_async_remote_copy(
            src_ref=grad.at[i],
            dst_ref=gin.at[me],
            send_sem=send_sem.at[4],
            recv_sem=g_sem,
            device_id=plane(i),
            device_id_type=MESH,
        ).start()
        pltpu.make_async_remote_copy(
            src_ref=gbias,
            dst_ref=gbin.at[me],
            send_sem=send_sem.at[5],
            recv_sem=gb_sem,
            device_id=plane(i),
            device_id_type=MESH,
        ).start()
        return carry

    lax.fori_loop(1, NP, scatter, 0)
    pltpu.make_async_copy(grad.at[me], gin.at[me], g_sem).start()
    pltpu.make_async_copy(gbias, gbin.at[me], gb_sem).start()
    pltpu.make_async_copy(gin, gin, g_sem).wait()
    pltpu.make_async_copy(gbin, gbin, gb_sem).wait()
    total, btotal = gin[0], gbin[0]
    for i in range(1, NP):
        total = total + gin[i]
        btotal = btotal + gbin[i]
    gsum[...] = total
    gbsum[...] = btotal

    def along(k, carry):
        t = (z + k) % NZ
        pltpu.make_async_remote_copy(
            src_ref=gsum,
            dst_ref=gzin.at[z],
            send_sem=send_sem.at[6],
            recv_sem=gz_sem,
            device_id=at_z(t),
            device_id_type=MESH,
        ).start()
        pltpu.make_async_remote_copy(
            src_ref=gbsum,
            dst_ref=gbzin.at[z],
            send_sem=send_sem.at[7],
            recv_sem=gbz_sem,
            device_id=at_z(t),
            device_id_type=MESH,
        ).start()
        return carry

    lax.fori_loop(1, NZ, along, 0)
    pltpu.make_async_copy(gsum, gzin.at[z], gz_sem).start()
    pltpu.make_async_copy(gbsum, gbzin.at[z], gbz_sem).start()
    pltpu.make_async_copy(gzin, gzin, gz_sem).wait()
    pltpu.make_async_copy(gbzin, gbzin, gbz_sem).wait()
    total, btotal = gzin[0], gbzin[0]
    for t in range(1, NZ):
        total = total + gzin[t]
        btotal = btotal + gbzin[t]
    gfin[...] = total
    gb_ref[...] = btotal

    def gather(k, carry):
        pltpu.make_async_remote_copy(
            src_ref=gfin,
            dst_ref=gall.at[me],
            send_sem=send_sem.at[8],
            recv_sem=ga_sem,
            device_id=plane((me + k) % NP),
            device_id_type=MESH,
        ).start()
        return carry

    lax.fori_loop(1, NP, gather, 0)
    pltpu.make_async_copy(gfin, gall.at[me], ga_sem).start()
    pltpu.make_async_copy(gall, gall, ga_sem).wait()
    grads_ref[...] = gall[...]

    def sent(n, ref):
        pltpu.make_async_copy(ref, ref, send_sem.at[n]).wait()

    sent(0, table.at[pl.ds(0, 2 * (2 * NZ - 1))])
    sent(1, idbox.at[pl.ds(0, NP - 1)])
    for _ in range(2):
        sent(2, inbox.at[0, pl.ds(0, NP - 1)])
    sent(3, zin.at[pl.ds(0, NZ - 1)])
    sent(4, gin.at[pl.ds(0, NP - 1)])
    sent(5, gbin.at[pl.ds(0, NP - 1)])
    sent(6, gzin.at[pl.ds(0, NZ - 1)])
    sent(7, gbzin.at[pl.ds(0, NZ - 1)])
    sent(8, gall.at[pl.ds(0, NP - 1)])


def hand_over(emb_ref, grads_ref, gb_ref, emb_out, gn_out, gs_out, gb_out):
    emb_out[...] = emb_ref[...]
    gn_out[...] = grads_ref[pl.ds(0, 16)].reshape(F, F)
    gs_out[...] = grads_ref[pl.ds(16, 16)].reshape(F, F)
    gb_out[...] = gb_ref[0]


def on_device(
    adj_tiles,
    tile_cols,
    send_block,
    send_count,
    history,
    node_feats,
    w_neigh,
    w_self,
    out_bias,
    cotangent,
):
    adj = adj_tiles.reshape(SLOTS, BLK, TPS * BLK)
    cols = tile_cols.reshape(SLOTS, TPS).T
    block = send_block.reshape(NP, 2).T
    count = send_count.reshape(1, NP)
    hist = history.reshape(2, BLK, F).transpose(1, 0, 2)
    any_spec = pl.BlockSpec(memory_space=pl.ANY)
    vmem_spec = pl.BlockSpec(memory_space=pltpu.VMEM)
    dma = pltpu.SemaphoreType.DMA
    emb, grads, gb = pl.pallas_call(
        body,
        out_shape=(
            jax.ShapeDtypeStruct(node_feats.shape, BF16),
            jax.ShapeDtypeStruct((NP, 8, F), F32),
            jax.ShapeDtypeStruct((1, F), F32),
        ),
        in_specs=[any_spec] * 10,
        out_specs=(vmem_spec,) * 3,
        scratch_shapes=[
            pltpu.SMEM((TPS, SLOTS), jnp.int32),
            pltpu.SMEM((2, NP), jnp.int32),
            pltpu.SMEM((1, NP), jnp.int32),
            pltpu.VMEM((SLOTS, BLK, TPS * BLK), BF16),
            pltpu.VMEM((BLK, 2, F), BF16),
            pltpu.VMEM((2 * NC * NZ, BLK, F), BF16),
            pltpu.VMEM((NC, 2, LANES), jnp.int32),
            pltpu.VMEM(node_feats.shape, BF16),
            pltpu.VMEM(node_feats.shape, BF16),
            pltpu.VMEM((F, F), BF16),
            pltpu.VMEM((F, F), BF16),
            pltpu.VMEM((1, F), F32),
            pltpu.VMEM((SLOTS // 2, BLK, F), F32),
            pltpu.VMEM((2, NP, NJ, 16, F), BF16),
            pltpu.VMEM((2, NP, NJ, 16, F), BF16),
            pltpu.VMEM((NP, 2, LANES), jnp.int32),
            pltpu.VMEM((2, HZ, NJ, OWN, F), BF16),
            pltpu.VMEM((NZ, NJ, OWN, F), BF16),
            pltpu.VMEM((NP, 8, F), F32),
            pltpu.VMEM((1, F), F32),
            pltpu.VMEM((NP, 8, F), F32),
            pltpu.VMEM((NP, 1, F), F32),
            pltpu.VMEM((8, F), F32),
            pltpu.VMEM((1, F), F32),
            pltpu.VMEM((NZ, 8, F), F32),
            pltpu.VMEM((NZ, 1, F), F32),
            pltpu.VMEM((8, F), F32),
            pltpu.VMEM((NP, 8, F), F32),
            dma((8,)),
            dma,
            dma,
            dma((NZ,)),
            dma,
            dma((9,)),
            dma((2,)),
            dma,
            dma,
            dma,
            dma,
            dma,
            dma,
            dma,
        ],
        compiler_params=pltpu.CompilerParams(collective_id=0, has_side_effects=True),
    )(
        cols,
        block,
        count,
        adj,
        hist,
        node_feats,
        cotangent,
        w_neigh,
        w_self,
        out_bias.reshape(1, F),
    )
    return pl.pallas_call(
        hand_over,
        out_shape=(
            jax.ShapeDtypeStruct(node_feats.shape, BF16),
            jax.ShapeDtypeStruct((F, F), F32),
            jax.ShapeDtypeStruct((F, F), F32),
            jax.ShapeDtypeStruct((F,), F32),
        ),
        in_specs=[vmem_spec] * 3,
        out_specs=(vmem_spec,) * 4,
    )(emb, grads, gb)


def solution(mesh):
    in_specs = (
        P("dst", "src", None, None, None),
        P("dst", "src", None, None),
        P("dst", "src", None, None),
        P("dst", "src", None),
        P("dst", "src", None),
        P("dst", "src"),
        P(),
        P(),
        P(),
        P("dst", "src"),
    )
    out_specs = (P("dst", "src"), P(), P(), P())
    return jax.shard_map(
        on_device, mesh=mesh, in_specs=in_specs, out_specs=out_specs, check_vma=False
    )
```

```python
import jax
import jax.numpy as jnp
from jax import lax
from jax.experimental import pallas as pl
from jax.experimental.pallas import tpu as pltpu
from jax.sharding import PartitionSpec as P

MESH = pl.DeviceIdType.MESH
NZ, NC, NS = 16, 2, 16
NP = NC * NS
BLK, F, TPS, SLOTS, OWN, NJ = 64, 128, 8, 64, 16, 4
HZ = NZ // 2
LANES = 128
TREE = (
    (0, (3, -3, 1, -1)),
    (3, (3, -1, 1)),
    (-3, (-3, 1, -1)),
    (6, (2, 1, -1)),
    (-6, (-1, 1)),
    (1, ()),
    (-1, ()),
    (2, ()),
    (-2, ()),
    (4, ()),
    (-4, ()),
    (5, ()),
    (-5, ()),
    (7, ()),
    (-7, ()),
    (8, ()),
)
LEVELS = ((0,), (3, -3), (6, -6), (1, -1, 2, -2, 4, -4, 5, -5, 7, -7, 8))
PIECE = 16
FIRST = (4, 12)
SEND_ORDER = ((4, 3, 5, 2, 6, 1, 7, 0), (0, 1, 7, 2, 6, 3, 5, 4))
NEAR = (1, -1, 2, -2, 3, -3)
F32, BF16 = jnp.float32, jnp.bfloat16


def body(
    cols_hbm,
    block_hbm,
    count_hbm,
    adj_hbm,
    hist_hbm,
    feats_hbm,
    cot_hbm,
    wn_hbm,
    ws_hbm,
    bias_hbm,
    emb_ref,
    grads_ref,
    gb_ref,
    cols,
    blocks,
    counts,
    adj,
    hist,
    table,
    ids,
    feats,
    cot,
    wn,
    ws,
    bias,
    part,
    outbox,
    inbox,
    idbox,
    zout,
    zin,
    grad,
    gbias,
    gin,
    gbin,
    gsum,
    gbsum,
    gzin,
    gbzin,
    gfin,
    gall,
    load_sem,
    adj_sem,
    table_sem,
    table_in,
    pair_in,
    send_sem,
    in_sem,
    id_sem,
    z_sem,
    g_sem,
    gb_sem,
    gz_sem,
    gbz_sem,
    ga_sem,
):
    d = lax.axis_index("dst")
    s = lax.axis_index("src")
    z = d // NC
    c = d % NC
    me = c * NS + s

    def plane(i):
        return (z * NC + i // NS, i % NS)

    def at_z(t):
        return (t * NC + c, s)

    def owner(h, i):
        return (z + FIRST[h] + i) % NZ

    small = [
        pltpu.make_async_copy(a, b, load_sem.at[n])
        for n, (a, b) in enumerate(
            (
                (cols_hbm, cols),
                (block_hbm, blocks),
                (count_hbm, counts),
                (feats_hbm, feats),
                (cot_hbm, cot),
                (wn_hbm, wn),
                (ws_hbm, ws),
                (bias_hbm, bias),
            )
        )
    ]
    own = pltpu.make_async_copy(hist_hbm, hist, table_sem)
    own.start()
    big = pltpu.make_async_copy(adj_hbm, adj, adj_sem)

    barrier = pltpu.get_barrier_semaphore()
    for off in NEAR:
        pl.semaphore_signal(
            barrier, inc=1, device_id=at_z((z + off + NZ) % NZ), device_id_type=MESH
        )

    def greet(k, carry):
        pl.semaphore_signal(
            barrier, inc=1, device_id=plane((me + k) % NP), device_id_type=MESH
        )
        return carry

    lax.fori_loop(1, NP, greet, 0)
    for op in small:
        op.start()
    big.start()
    own.wait()
    for g in range(2):
        table[d * 2 + g] = hist[:, g, :]
    for op in small[:3]:
        op.wait()
    lane_slot = lax.broadcasted_iota(jnp.int32, (1, LANES), 1) % 16
    for core in range(NC):
        for h in range(2):
            row = jnp.full((1, LANES), -1, jnp.int32)
            for n in range(16):
                k, i = n // HZ, n % HZ
                p = owner(h, i) * NC + core
                value = jnp.where(counts[0, p] > k, blocks[k, p] + i * OWN, -1)
                row = jnp.where(lane_slot == n, value, row)
            ids[core, pl.ds(h, 1), :] = row
    pl.semaphore_wait(barrier, NP - 1 + len(NEAR))

    slot_of = {off: n for n, (off, _) in enumerate(TREE)}

    def block(off, p):
        first = ((z - off + NZ) % NZ) * (2 * NC) + c * 2
        return table.at[pl.ds(first, 2), pl.ds(p * PIECE, PIECE)]

    def push(off, p, sem, device):
        pltpu.make_async_remote_copy(
            src_ref=block(off, p),
            dst_ref=block(off, p),
            send_sem=send_sem.at[0],
            recv_sem=sem,
            device_id=device,
            device_id_type=MESH,
        ).start()

    moves = dict(TREE)
    for level in LEVELS:
        for p in range(BLK // PIECE):
            for off in level:
                if off != 0:
                    pltpu.make_async_copy(
                        block(off, p), block(off, p), table_in.at[slot_of[off], p]
                    ).wait()
                for step in moves[off]:
                    push(
                        off,
                        p,
                        table_in.at[slot_of[off + step], p],
                        at_z((z + step + NZ) % NZ),
                    )
                push(off, p, pair_in, (z * NC + 1 - c, s))

    def send_ids(k, carry):
        i = (me + k) % NP
        pltpu.make_async_remote_copy(
            src_ref=ids.at[i // NS],
            dst_ref=idbox.at[me],
            send_sem=send_sem.at[1],
            recv_sem=id_sem,
            device_id=plane(i),
            device_id_type=MESH,
        ).start()
        return carry

    lax.fori_loop(1, NP, send_ids, 0)
    pltpu.make_async_copy(ids.at[c], idbox.at[me], id_sem).start()

    big.wait()
    pltpu.make_async_copy(
        table.at[pl.ds(0, 2 * NZ)], table.at[pl.ds(0, 2 * NZ)], pair_in
    ).wait()

    for h in range(2):

        def slot(n, carry):
            q = owner(h, n // 4) * 4 + n % 4
            picked = jnp.concatenate([table[cols[t, q]] for t in range(TPS)], axis=0)
            part[n] = jnp.dot(adj[q], picked, preferred_element_type=F32)
            return carry

        lax.fori_loop(0, SLOTS // 2, slot, 0, unroll=4)

        def pack(i, carry):
            for j in range(NJ):
                row = (i % NS) * NJ + j
                two = [
                    part[pl.ds((i // NS) * 2 + k, HZ, stride=4), row, :] for k in range(2)
                ]
                outbox[h, i, j] = jnp.concatenate(two, axis=0).astype(BF16)
            return carry

        lax.fori_loop(0, NP, pack, 0)

        def send(k, carry):
            i = (me + k) % NP
            pltpu.make_async_remote_copy(
                src_ref=outbox.at[h, i],
                dst_ref=inbox.at[h, me],
                send_sem=send_sem.at[2],
                recv_sem=in_sem.at[h],
                device_id=plane(i),
                device_id_type=MESH,
            ).start()
            return carry

        lax.fori_loop(1, NP, send, 0)
        pltpu.make_async_copy(outbox.at[h, me], inbox.at[h, me], in_sem.at[h]).start()

    for op in small[3:]:
        op.wait()

    pltpu.make_async_copy(idbox, idbox, id_sem).wait()
    lane_dev = lax.broadcasted_iota(jnp.int32, (1, LANES), 1) // 16
    row_id = lax.broadcasted_iota(jnp.int32, (LANES, LANES), 0)
    for h in range(2):
        parts = []
        for g in range(NP // 8):
            row = jnp.zeros((1, LANES), jnp.int32)
            for n in range(8):
                row = jnp.where(lane_dev == n, idbox[g * 8 + n, pl.ds(h, 1), :], row)
            parts.append((row_id == row).astype(F32).astype(BF16))
        chosen = jnp.concatenate(parts, axis=1)
        pltpu.make_async_copy(inbox.at[h], inbox.at[h], in_sem.at[h]).wait()
        for j in range(NJ):
            got = inbox[h, :, j].reshape(NP * 16, F)
            total = jnp.dot(chosen, got, preferred_element_type=F32)
            zout[h, :, j] = total.astype(BF16).reshape(HZ, OWN, F)
        for i in SEND_ORDER[h]:
            if FIRST[h] + i == NZ:
                pltpu.make_async_copy(zout.at[h, i], zin.at[z], z_sem).start()
            else:
                pltpu.make_async_remote_copy(
                    src_ref=zout.at[h, i],
                    dst_ref=zin.at[z],
                    send_sem=send_sem.at[3],
                    recv_sem=z_sem,
                    device_id=at_z(owner(h, i)),
                    device_id_type=MESH,
                ).start()

    pltpu.make_async_copy(zin, zin, z_sem).wait()

    aggs, selfs, grads_low = [], [], []
    gbias_sum = jnp.zeros((1, F), F32)
    for j in range(NJ):
        agg = zin[0, j].astype(F32)
        for t in range(1, NZ):
            agg = agg + zin[t, j].astype(F32)
        agg = agg.astype(BF16)
        mine = feats[:, j * F : (j + 1) * F]
        pre = (
            jnp.dot(agg, wn[...], preferred_element_type=F32)
            + jnp.dot(mine, ws[...], preferred_element_type=F32)
            + bias[...]
        )
        sig = jax.nn.sigmoid(pre)
        emb_ref[:, j * F : (j + 1) * F] = (pre * sig).astype(BF16)
        slope = sig * (1.0 + pre * (1.0 - sig))
        gpre = cot[:, j * F : (j + 1) * F].astype(F32) * slope * (float(NZ * NC * OWN * BLK) ** -0.5)
        gbias_sum = gbias_sum + jnp.sum(gpre, axis=0, keepdims=True)
        aggs.append(agg)
        selfs.append(mine)
        grads_low.append(gpre.astype(BF16))
    low = jnp.concatenate(grads_low, axis=0)
    for n, left in enumerate((aggs, selfs)):
        left = jnp.concatenate(left, axis=0)
        prod = lax.dot_general(
            left, low, (((0,), (0,)), ((), ())), preferred_element_type=F32
        )
        grad[pl.ds(n * 16, 16)] = prod.reshape(16, 8, F)
    gbias[...] = gbias_sum

    def scatter(k, carry):
        i = (me + k) % NP
        pltpu.make_async_remote_copy(
            src_ref=grad.at[i],
            dst_ref=gin.at[me],
            send_sem=send_sem.at[4],
            recv_sem=g_sem,
            device_id=plane(i),
            device_id_type=MESH,
        ).start()
        pltpu.make_async_remote_copy(
            src_ref=gbias,
            dst_ref=gbin.at[me],
            send_sem=send_sem.at[5],
            recv_sem=gb_sem,
            device_id=plane(i),
            device_id_type=MESH,
        ).start()
        return carry

    lax.fori_loop(1, NP, scatter, 0)
    pltpu.make_async_copy(grad.at[me], gin.at[me], g_sem).start()
    pltpu.make_async_copy(gbias, gbin.at[me], gb_sem).start()
    pltpu.make_async_copy(gin, gin, g_sem).wait()
    pltpu.make_async_copy(gbin, gbin, gb_sem).wait()
    total, btotal = gin[0], gbin[0]
    for i in range(1, NP):
        total = total + gin[i]
        btotal = btotal + gbin[i]
    gsum[...] = total
    gbsum[...] = btotal

    def along(n, carry):
        t = (z + HZ + (1 - 2 * (n % 2)) * ((n + 1) // 2) + NZ) % NZ
        pltpu.make_async_remote_copy(
            src_ref=gsum,
            dst_ref=gzin.at[z],
            send_sem=send_sem.at[6],
            recv_sem=gz_sem,
            device_id=at_z(t),
            device_id_type=MESH,
        ).start()
        pltpu.make_async_remote_copy(
            src_ref=gbsum,
            dst_ref=gbzin.at[z],
            send_sem=send_sem.at[7],
            recv_sem=gbz_sem,
            device_id=at_z(t),
            device_id_type=MESH,
        ).start()
        return carry

    lax.fori_loop(0, NZ - 1, along, 0)
    pltpu.make_async_copy(gsum, gzin.at[z], gz_sem).start()
    pltpu.make_async_copy(gbsum, gbzin.at[z], gbz_sem).start()
    pltpu.make_async_copy(gzin, gzin, gz_sem).wait()
    pltpu.make_async_copy(gbzin, gbzin, gbz_sem).wait()
    total, btotal = gzin[0], gbzin[0]
    for t in range(1, NZ):
        total = total + gzin[t]
        btotal = btotal + gbzin[t]
    gfin[...] = total
    gb_ref[...] = btotal

    def gather(k, carry):
        pltpu.make_async_remote_copy(
            src_ref=gfin,
            dst_ref=gall.at[me],
            send_sem=send_sem.at[8],
            recv_sem=ga_sem,
            device_id=plane((me + k) % NP),
            device_id_type=MESH,
        ).start()
        return carry

    lax.fori_loop(1, NP, gather, 0)
    pltpu.make_async_copy(gfin, gall.at[me], ga_sem).start()
    pltpu.make_async_copy(gall, gall, ga_sem).wait()
    grads_ref[...] = gall[...]

    def sent(n, ref):
        pltpu.make_async_copy(ref, ref, send_sem.at[n]).wait()

    sent(0, table.at[pl.ds(0, 2 * (2 * NZ - 1))])
    sent(1, idbox.at[pl.ds(0, NP - 1)])
    for _ in range(2):
        sent(2, inbox.at[0, pl.ds(0, NP - 1)])
    sent(3, zin.at[pl.ds(0, NZ - 1)])
    sent(4, gin.at[pl.ds(0, NP - 1)])
    sent(5, gbin.at[pl.ds(0, NP - 1)])
    sent(6, gzin.at[pl.ds(0, NZ - 1)])
    sent(7, gbzin.at[pl.ds(0, NZ - 1)])
    sent(8, gall.at[pl.ds(0, NP - 1)])


def hand_over(emb_ref, grads_ref, gb_ref, emb_out, gn_out, gs_out, gb_out):
    emb_out[...] = emb_ref[...]
    gn_out[...] = grads_ref[pl.ds(0, 16)].reshape(F, F)
    gs_out[...] = grads_ref[pl.ds(16, 16)].reshape(F, F)
    gb_out[...] = gb_ref[0]


def on_device(
    adj_tiles,
    tile_cols,
    send_block,
    send_count,
    history,
    node_feats,
    w_neigh,
    w_self,
    out_bias,
    cotangent,
):
    adj = adj_tiles.reshape(SLOTS, BLK, TPS * BLK)
    cols = tile_cols.reshape(SLOTS, TPS).T
    block = send_block.reshape(NP, 2).T
    count = send_count.reshape(1, NP)
    hist = history.reshape(2, BLK, F).transpose(1, 0, 2)
    any_spec = pl.BlockSpec(memory_space=pl.ANY)
    vmem_spec = pl.BlockSpec(memory_space=pltpu.VMEM)
    dma = pltpu.SemaphoreType.DMA
    emb, grads, gb = pl.pallas_call(
        body,
        out_shape=(
            pltpu.VMEM(node_feats.shape, BF16),
            pltpu.VMEM((NP, 8, F), F32),
            pltpu.VMEM((1, F), F32),
        ),
        in_specs=[any_spec] * 10,
        out_specs=(vmem_spec,) * 3,
        scratch_shapes=[
            pltpu.SMEM((TPS, SLOTS), jnp.int32),
            pltpu.SMEM((2, NP), jnp.int32),
            pltpu.SMEM((1, NP), jnp.int32),
            pltpu.VMEM((SLOTS, BLK, TPS * BLK), BF16),
            pltpu.VMEM((BLK, 2, F), BF16),
            pltpu.VMEM((2 * NC * NZ, BLK, F), BF16),
            pltpu.VMEM((NC, 2, LANES), jnp.int32),
            pltpu.VMEM(node_feats.shape, BF16),
            pltpu.VMEM(node_feats.shape, BF16),
            pltpu.VMEM((F, F), BF16),
            pltpu.VMEM((F, F), BF16),
            pltpu.VMEM((1, F), F32),
            pltpu.VMEM((SLOTS // 2, BLK, F), F32),
            pltpu.VMEM((2, NP, NJ, 16, F), BF16),
            pltpu.VMEM((2, NP, NJ, 16, F), BF16),
            pltpu.VMEM((NP, 2, LANES), jnp.int32),
            pltpu.VMEM((2, HZ, NJ, OWN, F), BF16),
            pltpu.VMEM((NZ, NJ, OWN, F), BF16),
            pltpu.VMEM((NP, 8, F), F32),
            pltpu.VMEM((1, F), F32),
            pltpu.VMEM((NP, 8, F), F32),
            pltpu.VMEM((NP, 1, F), F32),
            pltpu.VMEM((8, F), F32),
            pltpu.VMEM((1, F), F32),
            pltpu.VMEM((NZ, 8, F), F32),
            pltpu.VMEM((NZ, 1, F), F32),
            pltpu.VMEM((8, F), F32),
            pltpu.VMEM((NP, 8, F), F32),
            dma((8,)),
            dma,
            dma,
            dma((NZ, BLK // PIECE)),
            dma,
            dma((9,)),
            dma((2,)),
            dma,
            dma,
            dma,
            dma,
            dma,
            dma,
            dma,
        ],
        compiler_params=pltpu.CompilerParams(collective_id=0, has_side_effects=True),
    )(
        cols,
        block,
        count,
        adj,
        hist,
        node_feats,
        cotangent,
        w_neigh,
        w_self,
        out_bias.reshape(1, F),
    )
    return pl.pallas_call(
        hand_over,
        out_shape=(
            jax.ShapeDtypeStruct(node_feats.shape, BF16),
            jax.ShapeDtypeStruct((F, F), F32),
            jax.ShapeDtypeStruct((F, F), F32),
            jax.ShapeDtypeStruct((F,), F32),
        ),
        in_specs=[vmem_spec] * 3,
        out_specs=(vmem_spec,) * 4,
    )(*[pltpu.with_memory_space_constraint(x, pltpu.VMEM) for x in (emb, grads, gb)])


def solution(mesh):
    in_specs = (
        P("dst", "src", None, None, None),
        P("dst", "src", None, None),
        P("dst", "src", None, None),
        P("dst", "src", None),
        P("dst", "src", None),
        P("dst", "src"),
        P(),
        P(),
        P(),
        P("dst", "src"),
    )
    out_specs = (P("dst", "src"), P(), P(), P())
    return jax.shard_map(
        on_device, mesh=mesh, in_specs=in_specs, out_specs=out_specs, check_vma=False
    )
```
